512 devices in a mesh: ep: 64 (over z, x, core), tp: 8 (over y).
Axes of the slice: x: 4, y: 8, z: 8, core: 2. Of those that a mesh axis runs over, the one named last changes fastest.
Arguments:
- attn_out: bfloat16 [8192, 2048], P('ep', 'tp'), may hold values from -6 to 6
- resid: bfloat16 [8192, 2048], P(('ep', 'tp')), may hold values from -6 to 6
- norm_gain: float32 [2048], replicated, may hold values from 0.1 to 1.9
- expert_ids: int32 [8192, 6], P('ep'), may hold values from 0 to 63, all different within a row; in each aligned block of 128 rows (0 to 127, 128 to 255, ...) at most 16 rows name the same one
- gate_vals: float32 [8192, 6], P('ep'), may hold values from 0.1 to 1
- w_gate: bfloat16 [64, 1408, 2048], P('ep', 'tp'), may hold values from -0.125 to 0.125
- w_up: bfloat16 [64, 1408, 2048], P('ep', 'tp'), may hold values from -0.125 to 0.125
- w_down: bfloat16 [64, 1408, 2048], P('ep', 'tp'), may hold values from -0.15625 to 0.15625
Outputs:
- layer_out: bfloat16 [8192, 2048], P(('ep', 'tp'))
The draws below stay inside these ranges and needn't reach their ends.
Inputs may be any that keep to these rules, and one draw needn't show every extreme that they name: `expert_ids`: among the tokens of one index of ep (aligned blocks of 128 rows), no expert is chosen by more than 16 tokens; some expert reaches 16 in some blocks. The experts of one token differ.
All inputs are finite; a program needn't handle non-finite values.
Results may differ from the reference program's by a relative error of at most 0.0095.
Values may be sent and summed in bfloat16 or wider, within the bound.
A program may use at most 64 MiB of HBM per device.

```python
import math
import jax
import jax.numpy as jnp
import numpy as np
from jax import lax

D = 2048
FF = 1408
TOP = 6
TOK_EP = 128
EXPERTS = 64
TOKENS = 8192
CAP = 16
FF_DEV = 176
N_EP = 64
N_TP = 8


def block_levels(stream_key, extent, pieces, low, high):
    loudness, own = 1.0, jax.random.fold_in(stream_key, 6)
    for dim, parts in pieces:
        steps = jnp.exp(jax.random.uniform(jax.random.fold_in(own, dim), (parts,), jnp.float32, low / len(pieces), high / len(pieces)))
        loudness = loudness * jnp.repeat(steps, extent[dim] // parts).reshape([-1 if axis == dim else 1 for axis in range(len(extent))])
    return loudness


def shared_out(stream_key, own, number, rows, number_of, top, bound, skew):
    ranking = jax.random.permutation(stream_key, number_of)
    packed, usual = shares(number_of, rows * top, bound, skew, True), shares(number_of, rows * top, bound, skew, False)
    places = jnp.arange(number_of)

    def named(lengths, rotation):
        used = int((lengths > 0).sum())
        fixed = max(1, used // 4)
        passed = fixed + (places - fixed + rotation * (used - fixed)) % max(1, number_of - fixed)
        return jnp.zeros((number_of,), jnp.int32).at[ranking[jnp.where(places < fixed, places, passed)]].set(jnp.asarray(lengths, jnp.int32))

    lengths = jnp.where(number % 4 == 0, named(packed, number // 4), named(usual, number - number // 4 - 1))
    mixed = jax.random.permutation(jax.random.fold_in(own, 3), number_of)
    donor, sink = mixed[0:number_of // 2 * 2:2], mixed[1:number_of // 2 * 2:2]
    margin = jnp.minimum(lengths[donor] - 1, bound - lengths[sink]) // 2
    margin = jnp.where((donor == ranking[0]) | (sink == ranking[0]) | (lengths[sink] == 0), 0, jnp.maximum(margin, 0))
    passed = jax.random.randint(jax.random.fold_in(own, 4), (number_of // 2,), 0, 1 << 20) % (margin + 1)
    lengths = lengths.at[donor].add(-passed).at[sink].add(passed)
    labels = jnp.searchsorted(jnp.cumsum(lengths), jnp.arange(rows * top), side="right").astype(jnp.int32)
    table = labels.reshape(top, rows).T
    table = table[jax.random.permutation(jax.random.fold_in(own, 1), rows)]
    rotation = jax.random.randint(jax.random.fold_in(own, 2), (rows, 1), 0, top)
    return jnp.take_along_axis(table, (jnp.arange(top)[None, :] + rotation) % top, axis=1)


def shares(count, total, bound, slope, full):
    loads = [(1 << 20) // math.isqrt(standing ** slope) + 1 for standing in range(1, count + 1)]
    largest = bound if full else min(bound, max(-(-total // count), total * loads[0] // sum(loads)))
    least = 1 if total - largest >= count - 1 else 0
    counts, surplus = [largest] + [least] * (count - 1), total - largest - least * (count - 1)
    while surplus > 0:
        movable = [i for i in range(1, count) if counts[i] < largest] or [i for i in range(1, count) if counts[i] < bound]
        whole, remaining = sum([loads[i] for i in movable]), surplus
        for i in movable:
            addition = min(bound - counts[i], max(1, remaining * loads[i] // whole), surplus)
            counts[i] = counts[i] + addition
            surplus = surplus - addition
    return np.array(counts)


def bell_draw(stream_key, shape, width, most, shards=(), kind=jnp.bfloat16):
    result = width * jax.random.normal(stream_key, shape, jnp.float32)
    if shards:
        result = result * block_levels(stream_key, shape, shards, -0.22, 0.18)
    return jnp.clip(result, -most, most).astype(kind)


def setup_inputs(seed: int = 0) -> dict:
    key_list = jax.random.split(jax.random.key(seed), 9)
    attn_out = bell_draw(key_list[0], (TOKENS, D), 1.0, 6.0, ((0, 64), (1, 8)))
    resid = bell_draw(key_list[1], (TOKENS, D), 1.0, 6.0, ((0, 512),))
    norm_gain = jnp.clip(1.0 + 0.18 * jax.random.normal(key_list[2], (D,), jnp.float32), 0.1, 1.9)
    expert_ids_keys = jax.random.split(jax.random.fold_in(key_list[3], 1), TOKENS // TOK_EP)
    expert_ids_turns = jax.random.permutation(jax.random.fold_in(key_list[3], 3), TOKENS // TOK_EP)
    expert_ids = jax.vmap(lambda own, number: shared_out(jax.random.fold_in(key_list[3], 2), own, number, TOK_EP, EXPERTS, TOP, CAP, 1))(expert_ids_keys, expert_ids_turns).reshape((TOKENS, TOP))
    gate_vals = jnp.clip(jnp.exp(math.log(1.0) - 2.3025851 * jax.random.uniform(key_list[4], (TOKENS, TOP), jnp.float32) ** block_levels(key_list[4], (TOKENS, TOP), ((0, 64),), -0.2, 0.2)), 0.1, 1.0)
    w_gate = bell_draw(key_list[5], (EXPERTS, FF, D), D ** -0.5, 0.125, ((0, 64), (1, 8)))
    w_up = bell_draw(key_list[6], (EXPERTS, FF, D), D ** -0.5, 0.125, ((0, 64), (1, 8)))
    w_down = bell_draw(key_list[7], (EXPERTS, FF, D), FF ** -0.5, 0.15625, ((0, 64), (1, 8)))
    return dict(attn_out=attn_out, resid=resid, norm_gain=norm_gain, expert_ids=expert_ids, gate_vals=gate_vals, w_gate=w_gate, w_up=w_up, w_down=w_down)


def reference(attn_out, resid, norm_gain, expert_ids, gate_vals, w_gate, w_up, w_down):
    hidden_state = (resid.astype(jnp.float32) + attn_out.astype(jnp.float32)).astype(jnp.bfloat16)
    hidden_f32 = hidden_state.astype(jnp.float32)
    mean_sq = lax.optimization_barrier(jnp.mean(hidden_f32 * hidden_f32, axis=-1, keepdims=True))
    normed = (hidden_f32 * lax.rsqrt(mean_sq + 1e-05) * norm_gain.astype(jnp.float32)).astype(jnp.bfloat16)
    pairs = TOK_EP * TOP
    group_ids = expert_ids.reshape(N_EP, pairs).astype(jnp.int32)
    onehot = (group_ids[:, :, None] == jnp.arange(EXPERTS, dtype=jnp.int32)[None, None, :]).astype(jnp.int32)
    rank_in = lax.optimization_barrier(jnp.sum(onehot * (jnp.cumsum(onehot, axis=1) - onehot), axis=-1)).astype(jnp.int32)
    source = jnp.broadcast_to(jnp.arange(N_EP, dtype=jnp.int32)[:, None], (N_EP, pairs))
    token_of = (jnp.arange(N_EP, dtype=jnp.int32)[:, None] * TOK_EP + jnp.arange(pairs, dtype=jnp.int32)[None, :] // TOP).astype(jnp.int32)
    position = ((group_ids * N_EP + source) * CAP + rank_in).reshape(-1)
    table = jnp.full((EXPERTS * N_EP * CAP,), TOKENS, jnp.int32).at[position].set(token_of.reshape(-1))
    weight_table = jnp.zeros((EXPERTS * N_EP * CAP,), jnp.float32).at[position].set(gate_vals.reshape(-1).astype(jnp.float32))
    table = table.reshape(EXPERTS, N_EP * CAP)
    weight_table = weight_table.reshape(EXPERTS, N_EP * CAP)
    padded = jnp.concatenate([normed, jnp.zeros((1, D), jnp.bfloat16)], axis=0)

    def per_expert(carry, items):
        rows_idx, weights, gate_w, up_w, down_w = items
        rows = padded[rows_idx]
        gate_pre = jnp.dot(rows, gate_w.T, preferred_element_type=jnp.float32)
        up_pre = jnp.dot(rows, up_w.T, preferred_element_type=jnp.float32)
        act = (jax.nn.silu(gate_pre) * up_pre).astype(jnp.bfloat16)
        total = jnp.zeros((rows.shape[0], D), jnp.float32)
        for group in range(N_TP):
            part = jnp.dot(act[:, group * FF_DEV:(group + 1) * FF_DEV], down_w[group * FF_DEV:(group + 1) * FF_DEV], preferred_element_type=jnp.float32).astype(jnp.bfloat16)
            total = total + lax.optimization_barrier(part).astype(jnp.float32)
        slot_out = lax.optimization_barrier(total.astype(jnp.bfloat16)).astype(jnp.float32)
        carry = carry.at[rows_idx].add(weights[:, None] * slot_out)
        return (carry, None)
    moe, _ = lax.scan(per_expert, jnp.zeros((TOKENS + 1, D), jnp.float32), (table, weight_table, w_gate, w_up, w_down))
    return (hidden_f32 + moe[:TOKENS]).astype(jnp.bfloat16)
```

```python
import jax
import jax.numpy as jnp
from jax import lax
from jax.sharding import PartitionSpec as P

F32 = jnp.float32
BF16 = jnp.bfloat16


def per_device(attn_out, resid, norm_gain, expert_ids, gate_vals, w_gate, w_up, w_down):
    ep_count = lax.axis_size("ep")
    tok, top = expert_ids.shape
    cap = 4 * tok * top // (3 * ep_count)
    slots = ep_count * cap
    resid_cols = lax.all_to_all(resid, "tp", split_axis=1, concat_axis=0, tiled=True)
    down_cols = lax.all_to_all(w_down[0], "tp", split_axis=1, concat_axis=0, tiled=True)
    h = (resid_cols.astype(F32) + attn_out.astype(F32)).astype(BF16)
    hit = expert_ids[:, :, None] == jnp.arange(ep_count, dtype=jnp.int32)[None, None, :]
    chosen = jnp.any(hit, axis=1).astype(BF16)
    gates = jnp.sum(jnp.where(hit, gate_vals[:, :, None], 0.0), axis=1)
    earlier = jnp.tril(jnp.ones((tok, tok), BF16), -1)
    rank = jnp.dot(earlier, chosen, preferred_element_type=F32).astype(jnp.int32)
    place = (chosen[:, :, None] > 0) & (
        rank[:, :, None] == jnp.arange(cap, dtype=jnp.int32)[None, None, :]
    )
    weights = jnp.where(place, gates[:, :, None], 0.0).reshape(tok, slots)
    place = place.astype(BF16).reshape(tok, slots)
    send = lax.dot_general(place, h, (((0,), (0,)), ((), ())), preferred_element_type=F32).astype(BF16)
    got = lax.all_to_all(send.reshape(ep_count, cap, -1), "ep", split_axis=0, concat_axis=0, tiled=True)
    rows = lax.all_gather(got.reshape(slots, -1), "tp", axis=1, tiled=True)
    rows_f = rows.astype(F32)
    mean_sq = jnp.mean(rows_f * rows_f, axis=-1, keepdims=True)
    normed = (rows_f * lax.rsqrt(mean_sq + 1e-05) * norm_gain).astype(BF16)
    nt = (((1,), (1,)), ((), ()))
    gate_pre = lax.dot_general(w_gate[0], normed, nt, preferred_element_type=F32)
    up_pre = lax.dot_general(w_up[0], normed, nt, preferred_element_type=F32)
    act = (jax.nn.silu(gate_pre) * up_pre).astype(BF16)
    act_all = lax.all_gather(act, "tp", axis=0, tiled=True)
    out = lax.dot_general(
        act_all, down_cols, (((0,), (0,)), ((), ())), preferred_element_type=F32
    ).astype(BF16)
    back = lax.all_to_all(out.reshape(ep_count, cap, -1), "ep", split_axis=0, concat_axis=0, tiled=True)
    moe = jnp.dot(weights, back.reshape(slots, -1).astype(F32), precision=lax.Precision.HIGHEST)
    layer = (h.astype(F32) + moe).astype(BF16)
    return lax.all_to_all(layer, "tp", split_axis=0, concat_axis=1, tiled=True)


def solution(mesh):
    in_specs = (
        P("ep", "tp"),
        P(("ep", "tp"), None),
        P(),
        P("ep", None),
        P("ep", None),
        P("ep", "tp", None),
        P("ep", "tp", None),
        P("ep", "tp", None),
    )
    return jax.shard_map(
        per_device, mesh=mesh, in_specs=in_specs, out_specs=P(("ep", "tp"), None), check_vma=False
    )
```

```python
import functools

import jax
import jax.numpy as jnp
from jax import lax
from jax.experimental import pallas as pl
from jax.experimental.pallas import tpu as pltpu
from jax.sharding import PartitionSpec as P

F32 = jnp.float32
BF16 = jnp.bfloat16
MESH = pl.DeviceIdType.MESH
NT = (((1,), (1,)), ((), ()))
TN = (((0,), (0,)), ((), ()))


def ring_kernel(n, got, w_gate, w_up, w_down, gain, out, rows, acts, own_act, gate_acc, up_acc, sq_acc, out_acc,
                row_send, row_recv, act_send, act_recv):
    me = lax.axis_index("tp")
    after, before = lax.rem(me + 1, n), lax.rem(me + n - 1, n)
    half = n // 2
    width = got.shape[2]

    barrier = pltpu.get_barrier_semaphore()
    for neighbour in (before, after):
        pl.semaphore_signal(barrier, inc=1, device_id={"tp": neighbour}, device_id_type=MESH)
    pl.semaphore_wait(barrier, 2)

    def origin(way, hop):
        return lax.rem(me + n - hop, n) if way == 0 else lax.rem(me + hop, n)

    def copy(first, buf, send_sem, recv_sem, way, hop, chunk):
        src = first.at[chunk] if hop == 0 else buf.at[way, hop - 1, chunk]
        return pltpu.make_async_remote_copy(
            src_ref=src,
            dst_ref=buf.at[way, hop, chunk],
            send_sem=send_sem.at[way, hop, chunk],
            recv_sem=recv_sem.at[way, hop, chunk],
            device_id={"tp": after if way == 0 else before},
            device_id_type=MESH,
        )

    def travels(way, hop, chunk):
        return hop < half - 1 or (hop == half - 1 and chunk == way)

    def gather(first, buf, send_sem, recv_sem, use):
        make = functools.partial(copy, first, buf, send_sem, recv_sem)
        steps = [(way, chunk) for turn in range(2) for way, chunk in ((0, turn), (1, 1 - turn))]
        for way, chunk in steps:
            make(way, 0, chunk).start()
        use(first, me, (0, 1))
        for hop in range(1, half + 1):
            for pair in (steps[:2], steps[2:]):
                landed = [(way, chunk) for way, chunk in pair if travels(way, hop - 1, chunk)]
                for way, chunk in landed:
                    make(way, hop - 1, chunk).wait_recv()
                    if travels(way, hop, chunk):
                        make(way, hop, chunk).start()
                for way, chunk in landed:
                    use(buf.at[way, hop - 1], origin(way, hop), (chunk,))
        for hop in range(half):
            for way, chunk in steps:
                if travels(way, hop, chunk):
                    make(way, hop, chunk).wait_send()

    gate_acc[...] = jnp.zeros_like(gate_acc)
    up_acc[...] = jnp.zeros_like(up_acc)
    sq_acc[...] = jnp.zeros_like(sq_acc)
    ones = jnp.ones((8, width), BF16)

    def project(block, src, chunks):
        columns = pl.ds(pl.multiple_of(src * width, width), width)
        scale = gain[:, columns]
        gate_w = (w_gate[:, columns].astype(F32) * scale).astype(BF16)
        up_w = (w_up[:, columns].astype(F32) * scale).astype(BF16)
        for c in chunks:
            x = block[c]
            gate_acc[c] += lax.dot_general(gate_w, x, NT, preferred_element_type=F32)
            up_acc[c] += lax.dot_general(up_w, x, NT, preferred_element_type=F32)
            sq = x.astype(F32) * x.astype(F32)
            top = sq.astype(BF16)
            rest = (sq - top.astype(F32)).astype(BF16)
            sq_acc[c] += lax.dot_general(ones, top, NT, preferred_element_type=F32) + lax.dot_general(
                ones, rest, NT, preferred_element_type=F32)

    gather(got, rows, row_send, row_recv, project)

    for c in range(2):
        r = lax.rsqrt(sq_acc[c][:1] / (n * width) + 1e-05)
        g = gate_acc[c] * r
        own_act[c] = (g / (1.0 + jnp.exp(-g)) * (up_acc[c] * r)).astype(BF16)
    out_acc[...] = jnp.zeros_like(out_acc)

    def reduce(block, src, chunks):
        w = w_down[src]
        for c in chunks:
            out_acc[c] += lax.dot_general(block[c], w, TN, preferred_element_type=F32)

    gather(own_act, acts, act_send, act_recv, reduce)
    out[...] = out_acc[...].astype(BF16)


def experts(n, got, w_gate, w_up, w_down, gain):
    _, part, width = got.shape
    hidden = w_gate.shape[0]
    half = n // 2
    vmem = pl.BlockSpec(memory_space=pltpu.VMEM)
    sems = pltpu.SemaphoreType.DMA((2, half, 2))
    return pl.pallas_call(
        functools.partial(ring_kernel, n),
        out_shape=jax.ShapeDtypeStruct(got.shape, BF16),
        in_specs=[vmem] * 5,
        out_specs=vmem,
        scratch_shapes=[
            pltpu.VMEM((2, half, 2, part, width), BF16),
            pltpu.VMEM((2, half, 2, hidden, part), BF16),
            pltpu.VMEM((2, hidden, part), BF16),
            pltpu.VMEM((2, hidden, part), F32),
            pltpu.VMEM((2, hidden, part), F32),
            pltpu.VMEM((2, 8, part), F32),
            pltpu.VMEM((2, part, width), F32),
            sems, sems, sems, sems,
        ],
        compiler_params=pltpu.CompilerParams(collective_id=0, has_side_effects=True, vmem_limit_bytes=40 * 2**20),
    )(got, w_gate, w_up, w_down, gain)


def per_device(attn_out, resid, norm_gain, expert_ids, gate_vals, w_gate, w_up, w_down):
    ep_count = lax.axis_size("ep")
    tp_count = lax.axis_size("tp")
    tok, top = expert_ids.shape
    cap = 4 * tok * top // (3 * ep_count)
    slots = ep_count * cap
    resid_cols = lax.all_to_all(resid, "tp", split_axis=1, concat_axis=0, tiled=True)
    down_cols = lax.all_to_all(w_down[0], "tp", split_axis=1, concat_axis=0, tiled=True)
    h = (resid_cols.astype(F32) + attn_out.astype(F32)).astype(BF16)
    hit = expert_ids[:, :, None] == jnp.arange(ep_count, dtype=jnp.int32)[None, None, :]
    chosen = jnp.any(hit, axis=1).astype(BF16)
    gates = jnp.sum(jnp.where(hit, gate_vals[:, :, None], 0.0), axis=1)
    earlier = jnp.tril(jnp.ones((tok, tok), BF16), -1)
    rank = jnp.dot(earlier, chosen, preferred_element_type=F32).astype(jnp.int32)
    place = (chosen[:, :, None] > 0) & (
        rank[:, :, None] == jnp.arange(cap, dtype=jnp.int32)[None, None, :]
    )
    weights = jnp.where(place, gates[:, :, None], 0.0).reshape(tok, slots)
    place = place.astype(BF16).reshape(tok, slots)
    send = lax.dot_general(place, h, (((0,), (0,)), ((), ())), preferred_element_type=F32).astype(BF16)
    got = lax.all_to_all(send.reshape(ep_count, cap, -1), "ep", split_axis=0, concat_axis=0, tiled=True)
    out = experts(
        tp_count,
        got.reshape(2, slots // 2, -1),
        w_gate[0],
        w_up[0],
        down_cols.reshape(tp_count, w_down.shape[1], -1),
        norm_gain[None, :],
    )
    back = lax.all_to_all(out.reshape(ep_count, cap, -1), "ep", split_axis=0, concat_axis=0, tiled=True)
    moe = jnp.dot(weights, back.reshape(slots, -1).astype(F32), precision=lax.Precision.HIGHEST)
    layer = (h.astype(F32) + moe).astype(BF16)
    return lax.all_to_all(layer, "tp", split_axis=0, concat_axis=1, tiled=True)


def solution(mesh):
    in_specs = (
        P("ep", "tp"),
        P(("ep", "tp"), None),
        P(),
        P("ep", None),
        P("ep", None),
        P("ep", "tp", None),
        P("ep", "tp", None),
        P("ep", "tp", None),
    )
    return jax.shard_map(
        per_device, mesh=mesh, in_specs=in_specs, out_specs=P(("ep", "tp"), None), check_vma=False
    )
```

```python
import functools

import jax
import jax.numpy as jnp
from jax import lax
from jax.experimental import pallas as pl
from jax.experimental.pallas import tpu as pltpu
from jax.sharding import PartitionSpec as P

F32 = jnp.float32
BF16 = jnp.bfloat16
MESH = pl.DeviceIdType.MESH
NT = (((1,), (1,)), ((), ()))
TN = (((0,), (0,)), ((), ()))
GROUPS = 2


def expert_kernel(n_ep, n, send, w_gate, w_up, w_down, gain, back, got, down, scaled, rows, acts, own_act, result,
                  pre_acc, sq_acc, out_acc, local_sem, disp_send, disp_recv, down_send, down_recv, ret_send, ret_recv,
                  row_send, row_recv, act_send, act_recv):
    ep, me = lax.axis_index("ep"), lax.axis_index("tp")
    after, before = lax.rem(me + 1, n), lax.rem(me + n - 1, n)
    half = n // 2
    cap, width = send.shape[1:]
    hidden = w_gate.shape[0]
    per = n_ep // (2 * GROUPS)
    part = per * cap

    barrier = pltpu.get_barrier_semaphore()

    @pl.loop(1, n_ep)
    def _(i):
        pl.semaphore_signal(barrier, inc=1, device_id={"ep": lax.rem(ep + i, n_ep)}, device_id_type=MESH)

    for i in range(1, n):
        pl.semaphore_signal(barrier, inc=1, device_id={"tp": lax.rem(me + i, n)}, device_id_type=MESH)

    keep_rows = pltpu.make_async_copy(send.at[ep], got.at[0], local_sem.at[0])
    keep_rows.start()
    mine = pl.ds(pl.multiple_of(me * width, width), width)
    keep_down = pltpu.make_async_copy(w_down.at[:, mine], down.at[me], local_sem.at[1])
    keep_down.start()
    pl.semaphore_wait(barrier, n_ep - 1 + n - 1)

    def dispatch(i):
        to = lax.rem(ep + i, n_ep)
        return pltpu.make_async_remote_copy(
            src_ref=send.at[to], dst_ref=got.at[i], send_sem=disp_send.at[i], recv_sem=disp_recv.at[i],
            device_id={"ep": to}, device_id_type=MESH)

    def relay(i):
        to = lax.rem(me + i, n)
        columns = pl.ds(pl.multiple_of(to * width, width), width)
        return pltpu.make_async_remote_copy(
            src_ref=w_down.at[:, columns], dst_ref=down.at[me], send_sem=down_send.at[i], recv_sem=down_recv.at[i],
            device_id={"tp": to}, device_id_type=MESH)

    def give_back(p):
        return pltpu.make_async_remote_copy(
            src_ref=result.at[p], dst_ref=back.at[ep], send_sem=ret_send.at[p], recv_sem=ret_recv.at[p],
            device_id={"ep": lax.rem(ep + n_ep - p, n_ep)}, device_id_type=MESH)

    @pl.loop(1, n_ep)
    def _(i):
        dispatch(i).start()

    for i in range(1, n):
        relay(i).start()

    for s in range(n):
        columns = slice(s * width, (s + 1) * width)
        scale = gain[:, columns]
        scaled[s, :hidden] = (w_gate[:, columns].astype(F32) * scale).astype(BF16)
        scaled[s, hidden:] = (w_up[:, columns].astype(F32) * scale).astype(BF16)
    pre_acc[...] = jnp.zeros_like(pre_acc)
    sq_acc[...] = jnp.zeros_like(sq_acc)
    out_acc[...] = jnp.zeros_like(out_acc)
    ones = jnp.ones((8, width), BF16)

    def origin(way, hop):
        return lax.rem(me + n - hop, n) if way == 0 else lax.rem(me + hop, n)

    def travels(way, hop, c):
        return hop < half - 1 or (hop == half - 1 and c % 2 == way)

    class Ring:
        def __init__(self, first, buf, send_sem, recv_sem, use, group):
            self.first, self.buf, self.sems, self.use = first, buf, (send_sem, recv_sem), use
            a, b = 2 * group, 2 * group + 1
            self.pairs = [((0, a), (1, b)), ((0, b), (1, a))]

        def copy(self, way, hop, c):
            return pltpu.make_async_remote_copy(
                src_ref=self.first(c) if hop == 0 else self.buf.at[way, hop - 1, c],
                dst_ref=self.buf.at[way, hop, c],
                send_sem=self.sems[0].at[way, hop, c],
                recv_sem=self.sems[1].at[way, hop, c],
                device_id={"tp": after if way == 0 else before},
                device_id_type=MESH)

        def start(self):
            for pair in self.pairs:
                for way, c in pair:
                    if travels(way, 0, c):
                        self.copy(way, 0, c).start()

        def run(self, hook=None):
            for way, c in self.pairs[0]:
                self.use(self.first(c), me, c)
            if half == 1 and hook:
                hook()
            for hop in range(1, half + 1):
                for pair in self.pairs:
                    landed = [(way, c) for way, c in pair if travels(way, hop - 1, c)]
                    for way, c in landed:
                        self.copy(way, hop - 1, c).wait_recv()
                        if travels(way, hop, c):
                            self.copy(way, hop, c).start()
                    if hook and hop == half - 1 and pair is self.pairs[1]:
                        hook()
                    for way, c in landed:
                        self.use(self.buf.at[way, hop - 1, c], origin(way, hop), c)

        def drain(self):
            for hop in range(half):
                for pair in self.pairs:
                    for way, c in pair:
                        if travels(way, hop, c):
                            self.copy(way, hop, c).wait_send()

    def project(block, src, c):
        x = block[...].reshape(part, width)
        pre_acc[c] += lax.dot_general(scaled[src], x, NT, preferred_element_type=F32)
        sq = x.astype(F32) * x.astype(F32)
        top = sq.astype(BF16)
        rest = (sq - top.astype(F32)).astype(BF16)
        sq_acc[c] += lax.dot_general(ones, top, NT, preferred_element_type=F32) + lax.dot_general(
            ones, rest, NT, preferred_element_type=F32)

    def reduce(block, src, c):
        out_acc[c] += lax.dot_general(block[...], down[src], TN, preferred_element_type=F32)

    def activate(group):
        for c in (2 * group, 2 * group + 1):
            r = lax.rsqrt(sq_acc[c][:1] / (n * width) + 1e-05)
            g = pre_acc[c][:hidden] * r
            own_act[c] = (g / (1.0 + jnp.exp(-g)) * (pre_acc[c][hidden:] * r)).astype(BF16)

    def arrive(group):
        @pl.loop(max(1, 2 * per * group), 2 * per * (group + 1))
        def _(i):
            dispatch(i).wait_recv()

    row_rings = [Ring(lambda c: got.at[pl.ds(c * per, per)], rows, row_send, row_recv, project, g) for g in range(GROUPS)]
    act_rings = [Ring(lambda c: own_act.at[c], acts, act_send, act_recv, reduce, g) for g in range(GROUPS)]

    def begin_rows(group):
        arrive(group)
        row_rings[group].start()

    keep_rows.wait()
    begin_rows(0)
    for g in range(GROUPS):
        if g + 1 < GROUPS:
            row_rings[g].run(functools.partial(begin_rows, g + 1))
        else:
            row_rings[g].run(act_rings[0].start)
        activate(g)
    keep_down.wait()
    for i in range(1, n):
        relay(i).wait_recv()
    keep_result = pltpu.make_async_copy(result.at[0], back.at[ep], local_sem.at[2])
    for g in range(GROUPS):
        act_rings[g].run(act_rings[g + 1].start if g + 1 < GROUPS else None)
        for c in (2 * g, 2 * g + 1):
            result[c * per:(c + 1) * per] = out_acc[c].astype(BF16).reshape(per, cap, width)
        if g == 0:
            keep_result.start()

        @pl.loop(max(1, 2 * per * g), 2 * per * (g + 1))
        def _(p):
            give_back(p).start()

    for ring in row_rings + act_rings:
        ring.drain()
    for i in range(1, n):
        relay(i).wait_send()
    keep_result.wait()

    @pl.loop(1, n_ep)
    def _(i):
        dispatch(i).wait_send()
        give_back(i).wait_send()
        give_back(i).wait_recv()


def experts(n_ep, n, send, w_gate, w_up, w_down, gain):
    _, cap, width = send.shape
    hidden = w_gate.shape[0]
    half = n // 2
    chunks = 2 * GROUPS
    per = n_ep // chunks
    part = per * cap
    vmem = pl.BlockSpec(memory_space=pltpu.VMEM)
    dma = pltpu.SemaphoreType.DMA
    ring = dma((2, half, chunks))
    return pl.pallas_call(
        functools.partial(expert_kernel, n_ep, n),
        out_shape=jax.ShapeDtypeStruct(send.shape, BF16),
        in_specs=[vmem] * 5,
        out_specs=vmem,
        scratch_shapes=[
            pltpu.VMEM(send.shape, BF16),
            pltpu.VMEM((n, hidden, width), BF16),
            pltpu.VMEM((n, 2 * hidden, width), BF16),
            pltpu.VMEM((2, half, chunks, per, cap, width), BF16),
            pltpu.VMEM((2, half, chunks, hidden, part), BF16),
            pltpu.VMEM((chunks, hidden, part), BF16),
            pltpu.VMEM(send.shape, BF16),
            pltpu.VMEM((chunks, 2 * hidden, part), F32),
            pltpu.VMEM((chunks, 8, part), F32),
            pltpu.VMEM((chunks, part, width), F32),
            dma((3,)), dma((n_ep,)), dma((n_ep,)), dma((n,)), dma((n,)), dma((n_ep,)), dma((n_ep,)),
            ring, ring, ring, ring,
        ],
        compiler_params=pltpu.CompilerParams(collective_id=0, has_side_effects=True, vmem_limit_bytes=48 * 2**20),
    )(send, w_gate, w_up, w_down, gain)


def per_device(attn_out, resid, norm_gain, expert_ids, gate_vals, w_gate, w_up, w_down):
    ep_count = lax.axis_size("ep")
    tp_count = lax.axis_size("tp")
    tok, top = expert_ids.shape
    cap = 4 * tok * top // (3 * ep_count)
    slots = ep_count * cap
    resid_cols = lax.all_to_all(resid, "tp", split_axis=1, concat_axis=0, tiled=True)
    h = (resid_cols.astype(F32) + attn_out.astype(F32)).astype(BF16)
    hit = expert_ids[:, :, None] == jnp.arange(ep_count, dtype=jnp.int32)[None, None, :]
    chosen = jnp.any(hit, axis=1).astype(BF16)
    gates = jnp.sum(jnp.where(hit, gate_vals[:, :, None], 0.0), axis=1)
    earlier = jnp.tril(jnp.ones((tok, tok), BF16), -1)
    rank = jnp.dot(earlier, chosen, preferred_element_type=F32).astype(jnp.int32)
    place = (chosen[:, :, None] > 0) & (
        rank[:, :, None] == jnp.arange(cap, dtype=jnp.int32)[None, None, :]
    )
    weights = jnp.where(place, gates[:, :, None], 0.0).reshape(tok, slots)
    place = place.astype(BF16).reshape(tok, slots)
    send = lax.dot_general(place, h, (((0,), (0,)), ((), ())), preferred_element_type=F32).astype(BF16)
    back = experts(
        ep_count, tp_count, send.reshape(ep_count, cap, -1), w_gate[0], w_up[0], w_down[0], norm_gain[None, :]
    )
    moe = jnp.dot(weights, back.reshape(slots, -1).astype(F32), precision=lax.Precision.HIGHEST)
    layer = (h.astype(F32) + moe).astype(BF16)
    return lax.all_to_all(layer, "tp", split_axis=0, concat_axis=1, tiled=True)


def solution(mesh):
    in_specs = (
        P("ep", "tp"),
        P(("ep", "tp"), None),
        P(),
        P("ep", None),
        P("ep", None),
        P("ep", "tp", None),
        P("ep", "tp", None),
        P("ep", "tp", None),
    )
    return jax.shard_map(
        per_device, mesh=mesh, in_specs=in_specs, out_specs=P(("ep", "tp"), None), check_vma=False
    )
```

```python
import functools

import jax
import jax.numpy as jnp
from jax import lax
from jax.experimental import pallas as pl
from jax.experimental.pallas import tpu as pltpu
from jax.sharding import PartitionSpec as P

F32 = jnp.float32
BF16 = jnp.bfloat16
MESH = pl.DeviceIdType.MESH
NT = (((1,), (1,)), ((), ()))
TN = (((0,), (0,)), ((), ()))
GROUPS = 2


def layer_kernel(n_ep, n, cap, attn, resid, gain, ids, gates, w_gate, w_up, w_down, out, own_resid, h_buf, place, weights,
                 raw, send, got, down, scaled, rows, acts, own_act, result, back, pre_acc, sq_acc, out_acc, layer,
                 local_sem, res_send, res_recv, fin_send, fin_recv, disp_send, disp_recv, down_send, down_recv,
                 ret_send, ret_recv, row_send, row_recv, act_send, act_recv):
    ep, me = lax.axis_index("ep"), lax.axis_index("tp")
    after, before = lax.rem(me + 1, n), lax.rem(me + n - 1, n)
    half = n // 2
    tok, width = attn.shape
    top = ids.shape[1]
    slots = n_ep * cap
    hidden = w_gate.shape[0]
    per = n_ep // (2 * GROUPS)
    part = per * cap

    barrier = pltpu.get_barrier_semaphore()

    @pl.loop(1, n_ep)
    def _(i):
        pl.semaphore_signal(barrier, inc=1, device_id={"ep": lax.rem(ep + i, n_ep)}, device_id_type=MESH)

    for i in range(1, n):
        pl.semaphore_signal(barrier, inc=1, device_id={"tp": lax.rem(me + i, n)}, device_id_type=MESH)

    mine = pl.ds(pl.multiple_of(me * width, width), width)
    keep_resid = pltpu.make_async_copy(resid.at[:, mine], own_resid.at[me], local_sem.at[0])
    keep_down = pltpu.make_async_copy(w_down.at[:, mine], down.at[me], local_sem.at[1])
    load_gate = pltpu.make_async_copy(w_gate, raw.at[0], local_sem.at[2])
    load_up = pltpu.make_async_copy(w_up, raw.at[1], local_sem.at[3])
    for load in (keep_resid, load_gate, load_up, keep_down):
        load.start()

    def iota(shape, dim):
        return lax.broadcasted_iota(jnp.int32, shape, dim)

    ahead = iota((n_ep, slots), 0) - ep
    low = jnp.where(ahead < 0, ahead + n_ep, ahead) * cap
    slot = iota((n_ep, slots), 1)
    inside = (slot >= low) & (slot < low + cap)
    spread = jnp.where(inside, 1.0, 0.0).astype(BF16)
    nth = slot[:1].astype(F32) - jnp.sum(jnp.where(inside, low.astype(F32), 0.0), axis=0, keepdims=True)
    chosen = jnp.zeros((tok, n_ep), F32)
    gate = jnp.zeros((tok, n_ep), F32)
    for k in range(top):
        hit = ids[:, k:k + 1] == iota((tok, n_ep), 1)
        chosen += jnp.where(hit, 1.0, 0.0)
        gate += jnp.where(hit, gates[:, k:k + 1], 0.0)
    earlier = jnp.where(iota((tok, tok), 0) > iota((tok, tok), 1), 1.0, 0.0).astype(BF16)
    rank = jnp.dot(earlier, chosen.astype(BF16), preferred_element_type=F32)
    spot = jnp.where(chosen > 0, rank, float(tok)).astype(BF16)
    taken = jnp.dot(spot, spread, preferred_element_type=F32) == nth
    place[...] = jnp.where(taken, 1.0, 0.0).astype(BF16)
    rest = gate
    for term in range(3):
        piece = rest.astype(BF16)
        rest = rest - piece.astype(F32)
        wide = jnp.dot(piece, spread, preferred_element_type=F32)
        weights[term] = jnp.where(taken, wide, 0.0).astype(BF16)

    pl.semaphore_wait(barrier, n_ep - 1 + n - 1)

    def to_columns(i):
        to = lax.rem(me + i, n)
        columns = pl.ds(pl.multiple_of(to * width, width), width)
        return pltpu.make_async_remote_copy(
            src_ref=resid.at[:, columns], dst_ref=own_resid.at[me], send_sem=res_send.at[i], recv_sem=res_recv.at[i],
            device_id={"tp": to}, device_id_type=MESH)

    def to_rows(i):
        to = lax.rem(me + i, n)
        return pltpu.make_async_remote_copy(
            src_ref=layer.at[to], dst_ref=out.at[:, mine], send_sem=fin_send.at[i], recv_sem=fin_recv.at[i],
            device_id={"tp": to}, device_id_type=MESH)

    def dispatch(i):
        to = lax.rem(ep + i, n_ep)
        return pltpu.make_async_remote_copy(
            src_ref=send.at[i], dst_ref=got.at[i], send_sem=disp_send.at[i], recv_sem=disp_recv.at[i],
            device_id={"ep": to}, device_id_type=MESH)

    def relay(i):
        to = lax.rem(me + i, n)
        columns = pl.ds(pl.multiple_of(to * width, width), width)
        return pltpu.make_async_remote_copy(
            src_ref=w_down.at[:, columns], dst_ref=down.at[me], send_sem=down_send.at[i], recv_sem=down_recv.at[i],
            device_id={"tp": to}, device_id_type=MESH)

    def give_back(p):
        return pltpu.make_async_remote_copy(
            src_ref=result.at[p], dst_ref=back.at[p], send_sem=ret_send.at[p], recv_sem=ret_recv.at[p],
            device_id={"ep": lax.rem(ep + n_ep - p, n_ep)}, device_id_type=MESH)

    def blocks(group):
        return slice(2 * per * group, 2 * per * (group + 1))

    for i in range(1, n):
        to_columns(i).start()
    for i in range(1, n):
        relay(i).start()
    keep_resid.wait()
    for i in range(1, n):
        to_columns(i).wait_recv()
    h = (own_resid[...].reshape(tok, width).astype(F32) + attn[...].astype(F32)).astype(BF16)
    h_buf[...] = h
    keep_rows = pltpu.make_async_copy(send.at[0], got.at[0], local_sem.at[4])
    for g in range(GROUPS):
        x = lax.dot_general(place[:, 2 * part * g:2 * part * (g + 1)], h, TN, preferred_element_type=F32)
        send[blocks(g)] = x.astype(BF16).reshape(2 * per, cap, width)
        if g == 0:
            keep_rows.start()

        @pl.loop(max(1, 2 * per * g), 2 * per * (g + 1))
        def _(i):
            dispatch(i).start()

    load_gate.wait()
    load_up.wait()
    for s in range(n):
        columns = slice(s * width, (s + 1) * width)
        scale = gain[:, columns]
        scaled[s, :hidden] = (raw[0, :, columns].astype(F32) * scale).astype(BF16)
        scaled[s, hidden:] = (raw[1, :, columns].astype(F32) * scale).astype(BF16)
    pre_acc[...] = jnp.zeros_like(pre_acc)
    sq_acc[...] = jnp.zeros_like(sq_acc)
    out_acc[...] = jnp.zeros_like(out_acc)
    ones = jnp.ones((8, width), BF16)

    def origin(way, hop):
        return lax.rem(me + n - hop, n) if way == 0 else lax.rem(me + hop, n)

    def travels(way, hop, c):
        return hop < half - 1 or (hop == half - 1 and c % 2 == way)

    class Ring:
        def __init__(self, first, buf, send_sem, recv_sem, use, group):
            self.first, self.buf, self.sems, self.use = first, buf, (send_sem, recv_sem), use
            a, b = 2 * group, 2 * group + 1
            self.pairs = [((0, a), (1, b)), ((0, b), (1, a))]

        def copy(self, way, hop, c):
            return pltpu.make_async_remote_copy(
                src_ref=self.first(c) if hop == 0 else self.buf.at[way, hop - 1, c],
                dst_ref=self.buf.at[way, hop, c],
                send_sem=self.sems[0].at[way, hop, c],
                recv_sem=self.sems[1].at[way, hop, c],
                device_id={"tp": after if way == 0 else before},
                device_id_type=MESH)

        def start(self):
            for pair in self.pairs:
                for way, c in pair:
                    if travels(way, 0, c):
                        self.copy(way, 0, c).start()

        def run(self, hook=None):
            for way, c in self.pairs[0]:
                self.use(self.first(c), me, c)
            if half == 1 and hook:
                hook()
            for hop in range(1, half + 1):
                for pair in self.pairs:
                    landed = [(way, c) for way, c in pair if travels(way, hop - 1, c)]
                    for way, c in landed:
                        self.copy(way, hop - 1, c).wait_recv()
                        if travels(way, hop, c):
                            self.copy(way, hop, c).start()
                    if hook and hop == half - 1 and pair is self.pairs[1]:
                        hook()
                    for way, c in landed:
                        self.use(self.buf.at[way, hop - 1, c], origin(way, hop), c)

        def drain(self):
            for hop in range(half):
                for pair in self.pairs:
                    for way, c in pair:
                        if travels(way, hop, c):
                            self.copy(way, hop, c).wait_send()

    def project(block, src, c):
        x = block[...].reshape(part, width)
        pre_acc[c] += lax.dot_general(scaled[src], x, NT, preferred_element_type=F32)
        sq = x.astype(F32) * x.astype(F32)
        top = sq.astype(BF16)
        rest = (sq - top.astype(F32)).astype(BF16)
        sq_acc[c] += lax.dot_general(ones, top, NT, preferred_element_type=F32) + lax.dot_general(
            ones, rest, NT, preferred_element_type=F32)

    def reduce(block, src, c):
        out_acc[c] += lax.dot_general(block[...], down[src], TN, preferred_element_type=F32)

    def activate(group):
        for c in (2 * group, 2 * group + 1):
            r = lax.rsqrt(sq_acc[c][:1] / (n * width) + 1e-05)
            g = pre_acc[c][:hidden] * r
            own_act[c] = (g / (1.0 + jnp.exp(-g)) * (pre_acc[c][hidden:] * r)).astype(BF16)

    def arrive(group):
        @pl.loop(max(1, 2 * per * group), 2 * per * (group + 1))
        def _(i):
            dispatch(i).wait_recv()

    row_rings = [Ring(lambda c: got.at[pl.ds(c * per, per)], rows, row_send, row_recv, project, g) for g in range(GROUPS)]
    act_rings = [Ring(lambda c: own_act.at[c], acts, act_send, act_recv, reduce, g) for g in range(GROUPS)]

    def begin_rows(group):
        arrive(group)
        row_rings[group].start()

    keep_rows.wait()
    begin_rows(0)
    for g in range(GROUPS):
        if g + 1 < GROUPS:
            row_rings[g].run(functools.partial(begin_rows, g + 1))
        else:
            row_rings[g].run(act_rings[0].start)
        activate(g)
    keep_down.wait()
    for i in range(1, n):
        relay(i).wait_recv()
    keep_result = pltpu.make_async_copy(result.at[0], back.at[0], local_sem.at[5])
    for g in range(GROUPS):
        act_rings[g].run(act_rings[g + 1].start if g + 1 < GROUPS else None)
        for c in (2 * g, 2 * g + 1):
            result[c * per:(c + 1) * per] = out_acc[c].astype(BF16).reshape(per, cap, width)
        if g == 0:
            keep_result.start()

        @pl.loop(max(1, 2 * per * g), 2 * per * (g + 1))
        def _(p):
            give_back(p).start()

    moe = jnp.zeros((tok, width), F32)
    for g in range(GROUPS):
        if g == 0:
            keep_result.wait()

        @pl.loop(max(1, 2 * per * g), 2 * per * (g + 1))
        def _(p):
            give_back(p).wait_recv()

        x = back[blocks(g)].reshape(2 * part, width)
        for term in range(3):
            moe += jnp.dot(weights[term, :, 2 * part * g:2 * part * (g + 1)], x, preferred_element_type=F32)
    layer[...] = (h_buf[...].astype(F32) + moe).astype(BF16).reshape(layer.shape)
    keep_layer = pltpu.make_async_copy(layer.at[me], out.at[:, mine], local_sem.at[6])
    keep_layer.start()
    for i in range(1, n):
        to_rows(i).start()

    for ring in row_rings + act_rings:
        ring.drain()
    for i in range(1, n):
        relay(i).wait_send()
        to_columns(i).wait_send()

    @pl.loop(1, n_ep)
    def _(i):
        dispatch(i).wait_send()
        give_back(i).wait_send()

    keep_layer.wait()
    for i in range(1, n):
        to_rows(i).wait_send()
        to_rows(i).wait_recv()


def per_device(attn_out, resid, norm_gain, expert_ids, gate_vals, w_gate, w_up, w_down):
    n_ep, n = lax.axis_size("ep"), lax.axis_size("tp")
    tok, width = attn_out.shape
    hidden = w_gate.shape[1]
    cap = 4 * tok * expert_ids.shape[1] // (3 * n_ep)
    half = n // 2
    chunks = 2 * GROUPS
    per = n_ep // chunks
    part = per * cap
    vmem, anywhere = pl.BlockSpec(memory_space=pltpu.VMEM), pl.BlockSpec(memory_space=pl.ANY)
    dma = pltpu.SemaphoreType.DMA
    ring = dma((2, half, chunks))
    block = (n_ep, cap, width)
    return pl.pallas_call(
        functools.partial(layer_kernel, n_ep, n, cap),
        out_shape=jax.ShapeDtypeStruct(resid.shape, BF16),
        in_specs=[vmem] * 5 + [anywhere] * 3,
        out_specs=vmem,
        scratch_shapes=[
            pltpu.VMEM((n, tok // n, width), BF16),
            pltpu.VMEM((tok, width), BF16),
            pltpu.VMEM((tok, n_ep * cap), BF16),
            pltpu.VMEM((3, tok, n_ep * cap), BF16),
            pltpu.VMEM((2, hidden, n * width), BF16),
            pltpu.VMEM(block, BF16),
            pltpu.VMEM(block, BF16),
            pltpu.VMEM((n, hidden, width), BF16),
            pltpu.VMEM((n, 2 * hidden, width), BF16),
            pltpu.VMEM((2, half, chunks, per, cap, width), BF16),
            pltpu.VMEM((2, half, chunks, hidden, part), BF16),
            pltpu.VMEM((chunks, hidden, part), BF16),
            pltpu.VMEM(block, BF16),
            pltpu.VMEM(block, BF16),
            pltpu.VMEM((chunks, 2 * hidden, part), F32),
            pltpu.VMEM((chunks, 8, part), F32),
            pltpu.VMEM((chunks, part, width), F32),
            pltpu.VMEM((n, tok // n, width), BF16),
            dma((7,)), dma((n,)), dma((n,)), dma((n,)), dma((n,)), dma((n_ep,)), dma((n_ep,)), dma((n,)), dma((n,)),
            dma((n_ep,)), dma((n_ep,)), ring, ring, ring, ring,
        ],
        compiler_params=pltpu.CompilerParams(collective_id=0, has_side_effects=True, vmem_limit_bytes=48 * 2**20),
    )(attn_out, resid, norm_gain[None, :], expert_ids, gate_vals, w_gate[0], w_up[0], w_down[0])


def solution(mesh):
    in_specs = (
        P("ep", "tp"),
        P(("ep", "tp"), None),
        P(),
        P("ep", None),
        P("ep", None),
        P("ep", "tp", None),
        P("ep", "tp", None),
        P("ep", "tp", None),
    )
    return jax.shard_map(
        per_device, mesh=mesh, in_specs=in_specs, out_specs=P(("ep", "tp"), None), check_vma=False
    )
```

```python
import functools

import jax
import jax.numpy as jnp
from jax import lax
from jax.experimental import pallas as pl
from jax.experimental.pallas import tpu as pltpu
from jax.sharding import PartitionSpec as P

F32 = jnp.float32
BF16 = jnp.bfloat16
MESH = pl.DeviceIdType.MESH
NT = (((1,), (1,)), ((), ()))
TN = (((0,), (0,)), ((), ()))
GROUPS = 2


def layer_kernel(n_ep, n, cap, attn, resid, gain, ids, gates, w_gate, w_up, w_down, out, own_resid, h_buf, place, weights,
                 raw, send, got, down, scaled, rows, acts, own_act, result, back, pre_acc, sq_acc, out_acc, layer,
                 row_sem, local_sem, res_send, res_recv, fin_send, fin_recv, disp_send, disp_recv, down_send, down_recv,
                 ret_send, ret_recv, row_send, row_recv, act_send, act_recv):
    ep, me = lax.axis_index("ep"), lax.axis_index("tp")
    after, before = lax.rem(me + 1, n), lax.rem(me + n - 1, n)
    half = n // 2
    tok, width = attn.shape
    top = ids.shape[1]
    slots = n_ep * cap
    hidden = w_gate.shape[0]
    per = n_ep // (2 * GROUPS)
    part = per * cap

    barrier = pltpu.get_barrier_semaphore()

    count = max(1, n_ep // 4)
    row, place_in_row = lax.div(ep, count), lax.rem(ep, count)
    for i in range(1, count):
        pl.semaphore_signal(
            barrier, inc=1, device_id={"ep": row * count + lax.rem(place_in_row + i, count)}, device_id_type=MESH)
    column = [lax.rem(ep + i * count, n_ep) for i in range(1, n_ep // count)]
    for peer in column:
        pl.semaphore_signal(barrier, inc=1, device_id={"ep": peer}, device_id_type=MESH)
    for i in range(1, n):
        pl.semaphore_signal(barrier, inc=1, device_id={"tp": lax.rem(me + i, n)}, device_id_type=MESH)

    mine = pl.ds(pl.multiple_of(me * width, width), width)
    keep_resid = pltpu.make_async_copy(resid.at[:, mine], own_resid.at[me], local_sem.at[0])
    keep_down = pltpu.make_async_copy(w_down.at[:, mine], down.at[me], local_sem.at[1])
    load_gate = pltpu.make_async_copy(w_gate, raw.at[0], local_sem.at[2])
    load_up = pltpu.make_async_copy(w_up, raw.at[1], local_sem.at[3])
    for load in (keep_resid, load_gate, load_up, keep_down):
        load.start()

    def iota(shape, dim):
        return lax.broadcasted_iota(jnp.int32, shape, dim)

    ahead = iota((n_ep, slots), 0) - ep
    low = jnp.where(ahead < 0, ahead + n_ep, ahead) * cap
    slot = iota((n_ep, slots), 1)
    inside = (slot >= low) & (slot < low + cap)
    spread = jnp.where(inside, 1.0, 0.0).astype(BF16)
    nth = slot[:1].astype(F32) - jnp.sum(jnp.where(inside, low.astype(F32), 0.0), axis=0, keepdims=True)
    chosen = jnp.zeros((tok, n_ep), F32)
    gate = jnp.zeros((tok, n_ep), F32)
    for k in range(top):
        hit = ids[:, k:k + 1] == iota((tok, n_ep), 1)
        chosen += jnp.where(hit, 1.0, 0.0)
        gate += jnp.where(hit, gates[:, k:k + 1], 0.0)
    earlier = jnp.where(iota((tok, tok), 0) > iota((tok, tok), 1), 1.0, 0.0).astype(BF16)
    rank = jnp.dot(earlier, chosen.astype(BF16), preferred_element_type=F32)
    spot = jnp.where(chosen > 0, rank, float(tok)).astype(BF16)
    taken = jnp.dot(spot, spread, preferred_element_type=F32) == nth
    place[...] = jnp.where(taken, 1.0, 0.0).astype(BF16)
    rest = gate
    for term in range(3):
        piece = rest.astype(BF16)
        rest = rest - piece.astype(F32)
        wide = jnp.dot(piece, spread, preferred_element_type=F32)
        weights[term] = jnp.where(taken, wide, 0.0).astype(BF16)

    pl.semaphore_wait(barrier, count - 1 + len(column) + n - 1)
    for peer in column:
        pl.semaphore_signal(row_sem, inc=1, device_id={"ep": peer}, device_id_type=MESH)

    def to_columns(i):
        to = lax.rem(me + i, n)
        columns = pl.ds(pl.multiple_of(to * width, width), width)
        return pltpu.make_async_remote_copy(
            src_ref=resid.at[:, columns], dst_ref=own_resid.at[me], send_sem=res_send.at[i], recv_sem=res_recv.at[i],
            device_id={"tp": to}, device_id_type=MESH)

    def to_rows(i):
        to = lax.rem(me + i, n)
        return pltpu.make_async_remote_copy(
            src_ref=layer.at[to], dst_ref=out.at[:, mine], send_sem=fin_send.at[i], recv_sem=fin_recv.at[i],
            device_id={"tp": to}, device_id_type=MESH)

    def dispatch(i):
        to = lax.rem(ep + i, n_ep)
        return pltpu.make_async_remote_copy(
            src_ref=send.at[i], dst_ref=got.at[i], send_sem=disp_send.at[i], recv_sem=disp_recv.at[i],
            device_id={"ep": to}, device_id_type=MESH)

    def relay(i):
        to = lax.rem(me + i, n)
        columns = pl.ds(pl.multiple_of(to * width, width), width)
        return pltpu.make_async_remote_copy(
            src_ref=w_down.at[:, columns], dst_ref=down.at[me], send_sem=down_send.at[i], recv_sem=down_recv.at[i],
            device_id={"tp": to}, device_id_type=MESH)

    def give_back(p):
        return pltpu.make_async_remote_copy(
            src_ref=result.at[p], dst_ref=back.at[p], send_sem=ret_send.at[p], recv_sem=ret_recv.at[p],
            device_id={"ep": lax.rem(ep + n_ep - p, n_ep)}, device_id_type=MESH)

    def blocks(group):
        return slice(2 * per * group, 2 * per * (group + 1))

    for i in range(1, n):
        to_columns(i).start()
    for i in range(1, n):
        relay(i).start()
    keep_resid.wait()
    for i in range(1, n):
        to_columns(i).wait_recv()
    h = (own_resid[...].reshape(tok, width).astype(F32) + attn[...].astype(F32)).astype(BF16)
    h_buf[...] = h
    keep_rows = pltpu.make_async_copy(send.at[0], got.at[0], local_sem.at[4])
    for g in range(GROUPS):
        x = lax.dot_general(place[:, 2 * part * g:2 * part * (g + 1)], h, TN, preferred_element_type=F32)
        send[blocks(g)] = x.astype(BF16).reshape(2 * per, cap, width)
        if g == 0:
            keep_rows.start()
            pl.semaphore_wait(row_sem, len(column))

        @pl.loop(max(1, 2 * per * g), 2 * per * (g + 1))
        def _(i):
            dispatch(i).start()

    load_gate.wait()
    load_up.wait()
    for s in range(n):
        columns = slice(s * width, (s + 1) * width)
        scale = gain[:, columns]
        scaled[s, :hidden] = (raw[0, :, columns].astype(F32) * scale).astype(BF16)
        scaled[s, hidden:] = (raw[1, :, columns].astype(F32) * scale).astype(BF16)
    pre_acc[...] = jnp.zeros_like(pre_acc)
    sq_acc[...] = jnp.zeros_like(sq_acc)
    out_acc[...] = jnp.zeros_like(out_acc)
    ones = jnp.ones((8, width), BF16)

    def origin(way, hop):
        return lax.rem(me + n - hop, n) if way == 0 else lax.rem(me + hop, n)

    def travels(way, hop, c):
        return hop < half - 1 or (hop == half - 1 and c % 2 == way)

    class Ring:
        def __init__(self, first, buf, send_sem, recv_sem, use, group):
            self.first, self.buf, self.sems, self.use = first, buf, (send_sem, recv_sem), use
            a, b = 2 * group, 2 * group + 1
            self.pairs = [((0, a), (1, b)), ((0, b), (1, a))]

        def copy(self, way, hop, c):
            return pltpu.make_async_remote_copy(
                src_ref=self.first(c) if hop == 0 else self.buf.at[way, hop - 1, c],
                dst_ref=self.buf.at[way, hop, c],
                send_sem=self.sems[0].at[way, hop, c],
                recv_sem=self.sems[1].at[way, hop, c],
                device_id={"tp": after if way == 0 else before},
                device_id_type=MESH)

        def start(self):
            for pair in self.pairs:
                for way, c in pair:
                    if travels(way, 0, c):
                        self.copy(way, 0, c).start()

        def run(self, hook=None):
            for way, c in self.pairs[0]:
                self.use(self.first(c), me, c)
            if half == 1 and hook:
                hook()
            for hop in range(1, half + 1):
                for pair in self.pairs:
                    landed = [(way, c) for way, c in pair if travels(way, hop - 1, c)]
                    for way, c in landed:
                        self.copy(way, hop - 1, c).wait_recv()
                        if travels(way, hop, c):
                            self.copy(way, hop, c).start()
                    if hook and hop == half - 1 and pair is self.pairs[1]:
                        hook()
                    for way, c in landed:
                        self.use(self.buf.at[way, hop - 1, c], origin(way, hop), c)

        def drain(self):
            for hop in range(half):
                for pair in self.pairs:
                    for way, c in pair:
                        if travels(way, hop, c):
                            self.copy(way, hop, c).wait_send()

    def project(block, src, c):
        x = block[...].reshape(part, width)
        pre_acc[c] += lax.dot_general(scaled[src], x, NT, preferred_element_type=F32)
        sq = x.astype(F32) * x.astype(F32)
        top = sq.astype(BF16)
        rest = (sq - top.astype(F32)).astype(BF16)
        sq_acc[c] += lax.dot_general(ones, top, NT, preferred_element_type=F32) + lax.dot_general(
            ones, rest, NT, preferred_element_type=F32)

    def reduce(block, src, c):
        out_acc[c] += lax.dot_general(block[...], down[src], TN, preferred_element_type=F32)

    def activate(group):
        for c in (2 * group, 2 * group + 1):
            r = lax.rsqrt(sq_acc[c][:1] / (n * width) + 1e-05)
            g = pre_acc[c][:hidden] * r
            own_act[c] = (g / (1.0 + jnp.exp(-g)) * (pre_acc[c][hidden:] * r)).astype(BF16)

    def arrive(group):
        @pl.loop(max(1, 2 * per * group), 2 * per * (group + 1))
        def _(i):
            dispatch(i).wait_recv()

    row_rings = [Ring(lambda c: got.at[pl.ds(c * per, per)], rows, row_send, row_recv, project, g) for g in range(GROUPS)]
    act_rings = [Ring(lambda c: own_act.at[c], acts, act_send, act_recv, reduce, g) for g in range(GROUPS)]

    def begin_rows(group):
        arrive(group)
        row_rings[group].start()

    keep_rows.wait()
    begin_rows(0)
    for g in range(GROUPS):
        if g + 1 < GROUPS:
            row_rings[g].run(functools.partial(begin_rows, g + 1))
        else:
            row_rings[g].run(act_rings[0].start)
        activate(g)
    keep_down.wait()
    for i in range(1, n):
        relay(i).wait_recv()
    keep_result = pltpu.make_async_copy(result.at[0], back.at[0], local_sem.at[5])
    for g in range(GROUPS):
        act_rings[g].run(act_rings[g + 1].start if g + 1 < GROUPS else None)
        for c in (2 * g, 2 * g + 1):
            result[c * per:(c + 1) * per] = out_acc[c].astype(BF16).reshape(per, cap, width)
        if g == 0:
            keep_result.start()

        @pl.loop(max(1, 2 * per * g), 2 * per * (g + 1))
        def _(p):
            give_back(p).start()

    moe = jnp.zeros((tok, width), F32)
    for g in range(GROUPS):
        if g == 0:
            keep_result.wait()

        @pl.loop(max(1, 2 * per * g), 2 * per * (g + 1))
        def _(p):
            give_back(p).wait_recv()

        x = back[blocks(g)].reshape(2 * part, width)
        for term in range(3):
            moe += jnp.dot(weights[term, :, 2 * part * g:2 * part * (g + 1)], x, preferred_element_type=F32)
    layer[...] = (h_buf[...].astype(F32) + moe).astype(BF16).reshape(layer.shape)
    keep_layer = pltpu.make_async_copy(layer.at[me], out.at[:, mine], local_sem.at[6])
    keep_layer.start()
    for i in range(1, n):
        to_rows(i).start()

    for ring in row_rings + act_rings:
        ring.drain()
    for i in range(1, n):
        relay(i).wait_send()
        to_columns(i).wait_send()

    @pl.loop(1, n_ep)
    def _(i):
        dispatch(i).wait_send()
        give_back(i).wait_send()

    keep_layer.wait()
    for i in range(1, n):
        to_rows(i).wait_send()
        to_rows(i).wait_recv()


def per_device(attn_out, resid, norm_gain, expert_ids, gate_vals, w_gate, w_up, w_down):
    n_ep, n = lax.axis_size("ep"), lax.axis_size("tp")
    tok, width = attn_out.shape
    hidden = w_gate.shape[1]
    cap = 4 * tok * expert_ids.shape[1] // (3 * n_ep)
    half = n // 2
    chunks = 2 * GROUPS
    per = n_ep // chunks
    part = per * cap
    vmem, anywhere = pl.BlockSpec(memory_space=pltpu.VMEM), pl.BlockSpec(memory_space=pl.ANY)
    dma = pltpu.SemaphoreType.DMA
    ring = dma((2, half, chunks))
    block = (n_ep, cap, width)
    return pl.pallas_call(
        functools.partial(layer_kernel, n_ep, n, cap),
        out_shape=jax.ShapeDtypeStruct(resid.shape, BF16),
        in_specs=[vmem] * 5 + [anywhere] * 3,
        out_specs=vmem,
        scratch_shapes=[
            pltpu.VMEM((n, tok // n, width), BF16),
            pltpu.VMEM((tok, width), BF16),
            pltpu.VMEM((tok, n_ep * cap), BF16),
            pltpu.VMEM((3, tok, n_ep * cap), BF16),
            pltpu.VMEM((2, hidden, n * width), BF16),
            pltpu.VMEM(block, BF16),
            pltpu.VMEM(block, BF16),
            pltpu.VMEM((n, hidden, width), BF16),
            pltpu.VMEM((n, 2 * hidden, width), BF16),
            pltpu.VMEM((2, half, chunks, per, cap, width), BF16),
            pltpu.VMEM((2, half, chunks, hidden, part), BF16),
            pltpu.VMEM((chunks, hidden, part), BF16),
            pltpu.VMEM(block, BF16),
            pltpu.VMEM(block, BF16),
            pltpu.VMEM((chunks, 2 * hidden, part), F32),
            pltpu.VMEM((chunks, 8, part), F32),
            pltpu.VMEM((chunks, part, width), F32),
            pltpu.VMEM((n, tok // n, width), BF16),
            pltpu.SemaphoreType.REGULAR, dma((7,)), dma((n,)), dma((n,)), dma((n,)), dma((n,)), dma((n_ep,)), dma((n_ep,)), dma((n,)), dma((n,)),
            dma((n_ep,)), dma((n_ep,)), ring, ring, ring, ring,
        ],
        compiler_params=pltpu.CompilerParams(collective_id=0, has_side_effects=True, vmem_limit_bytes=48 * 2**20),
    )(attn_out, resid, norm_gain[None, :], expert_ids, gate_vals, w_gate[0], w_up[0], w_down[0])


def solution(mesh):
    in_specs = (
        P("ep", "tp"),
        P(("ep", "tp"), None),
        P(),
        P("ep", None),
        P("ep", None),
        P("ep", "tp", None),
        P("ep", "tp", None),
        P("ep", "tp", None),
    )
    return jax.shard_map(
        per_device, mesh=mesh, in_specs=in_specs, out_specs=P(("ep", "tp"), None), check_vma=False
    )
```
